32 devices in a mesh: tm: 2 (over core), loan: 8 (over z, y), cov: 2 (over x).
Axes of the slice: x: 2, y: 2, z: 4, core: 2. Of those that a mesh axis runs over, the one named last changes fastest.
Arguments:
- covars: float32 [65536, 1024], P(('tm', 'loan'), 'cov'), may hold values from -6 to 6
- events: int32 [65536], P(('tm', 'loan')), may hold values 0 or 1
- group: int32 [65536], P(('tm', 'loan')), may hold values from 0 to 511, as said below
- counts: int32 [16], P(('tm', 'loan')), may hold values from 1024 to 4096
- beta: float32 [1024], P('cov'), may hold values from -0.1875 to 0.1875
- vecs: float32 [2, 1024], P(None, 'cov'), may hold values from -12 to 12
Outputs:
- hessvec: float32 [2, 1024], P(None, 'cov')
The draws below stay inside these ranges and needn't reach their ends.
Inputs may be any that keep to these rules, and one draw needn't show every extreme that they name: `group`: block b holds tie groups of time shard b // (16 // (512 // 256)) only: from 256 times the shard's index to 256 more minus one; the first 256 rows of every block hold each of these groups once.
All inputs are finite; a program needn't handle non-finite values. No bound on the sum of `events` on one device may be relied on, other than what follows from the above.
Results may differ from the reference program's by a relative error of at most 0.00028.
Values sent between devices are 32-bit elements; how exact they have to be, the bound alone decides.
No kernel may reach another device: no remote copies, remote signals or barrier semaphores. Data moves between devices by JAX's collectives and lax.ppermute only.
A program may use at most 64 MiB of HBM per device.

```python
import jax
import jax.numpy as jnp
from jax import lax

P_SIZE = 1024
ROWS = 4096
G_SH = 256
BLOCKS = 16
RECORDS = 65536
GROUPS = 512


def draw_covars(key, part):
    first_key, second_key = jax.random.split(jax.random.fold_in(key, 11))
    noise = jnp.clip(jax.random.normal(first_key, (RECORDS, P_SIZE), jnp.float32), -4.5, 4.5)
    centre = jax.random.uniform(second_key, (P_SIZE,), jnp.float32, -1.0, 1.0)
    return noise + centre[None, :]


def draw_group(key, part):
    index = jnp.arange(RECORDS, dtype=jnp.int32)
    position = index % ROWS
    per_shard = RECORDS // (GROUPS // G_SH)
    shard = index // per_shard
    picked = jax.random.randint(jax.random.fold_in(key, 23), (RECORDS,), 0, G_SH, dtype=jnp.int32)
    local = jnp.where(position < G_SH, position, picked)
    return (shard * G_SH + local).astype(jnp.int32)


def draw_counts(key, part):
    first_key, second_key = jax.random.split(jax.random.fold_in(key, 37))
    drawn = jax.random.randint(first_key, (BLOCKS,), ROWS // 4, ROWS + 1, dtype=jnp.int32)
    fullest = jax.random.randint(second_key, (), 0, BLOCKS, dtype=jnp.int32)
    return jnp.where(jnp.arange(BLOCKS, dtype=jnp.int32) == fullest, ROWS, drawn).astype(jnp.int32)


def touch_ends(values, stream_key, least, largest):
    index_at = [jax.random.randint(jax.random.fold_in(stream_key, axis), (), 0, length) for axis, length in enumerate(values.shape)]
    longest = values.shape.index(max(values.shape))
    neighbour = index_at[:longest] + [(index_at[longest] + 1) % values.shape[longest]] + index_at[longest + 1:]
    return values.at[tuple(index_at)].set(least).at[tuple(neighbour)].set(largest)


def block_levels(stream_key, shape, cuts, least, largest):
    level = 1.0
    for axis_at, blocks in cuts:
        steps = jax.random.uniform(jax.random.fold_in(jax.random.fold_in(stream_key, 6), axis_at), (blocks,), jnp.float32, least / len(cuts), largest / len(cuts))
        level = level * jnp.repeat(jnp.exp(steps), shape[axis_at] // blocks).reshape((-1,) + (1,) * (len(shape) - 1 - axis_at))
    return level


def gaussian(own_key, dims, scale, limit, cuts=(), kind=jnp.bfloat16):
    entries = scale * jax.random.normal(own_key, dims, jnp.float32)
    if cuts:
        entries = entries * block_levels(own_key, dims, cuts, -0.22, 0.18)
    return jnp.clip(entries, -limit, limit).astype(kind)


def setup_inputs(seed: int = 0) -> dict:
    key_list = jax.random.split(jax.random.key(seed), 7)
    return {
        "covars": draw_covars(jax.random.fold_in(key_list[6], 71), 0),
        "events": touch_ends((jax.random.randint(key_list[1], (RECORDS,), 0, 3) < 1).astype(jnp.int32), jax.random.fold_in(key_list[1], 1), 0, 1),
        "group": draw_group(jax.random.fold_in(key_list[6], 71), 0),
        "counts": draw_counts(jax.random.fold_in(key_list[6], 71), 0),
        "beta": gaussian(key_list[4], (P_SIZE,), P_SIZE ** -0.5, 0.1875, ((0, 2),), jnp.float32),
        "vecs": gaussian(key_list[5], (2, P_SIZE), 2.0, 12.0, ((1, 2),), jnp.float32),
    }


def reference(covars, events, group, counts, beta, vecs):
    total = covars.shape[0]
    index = jnp.arange(total, dtype=jnp.int32)
    position = index % ROWS
    block_of = index // ROWS
    valid = (position < counts[block_of]).astype(jnp.float32)
    coeffs = jnp.concatenate([beta[None, :], vecs], axis=0)
    linear = jnp.dot(covars, coeffs.T, precision=lax.Precision.HIGHEST)
    weight = valid * jnp.exp(linear[:, 0])
    proj = linear[:, 1:3]
    died = valid * events.astype(jnp.float32)
    per_record = jnp.concatenate([weight[:, None], weight[:, None] * proj, died[:, None]], axis=1)
    sums = jax.ops.segment_sum(per_record, group, num_segments=GROUPS)
    tail = jnp.cumsum(sums[::-1, :3], axis=0)[::-1]
    risk0 = tail[:, 0]
    riskproj = tail[:, 1:3]
    died_grp = sums[:, 3]
    first = jnp.cumsum(died_grp / risk0)
    second = jnp.cumsum(died_grp[:, None] * riskproj / (risk0 * risk0)[:, None], axis=0)
    resid = weight[:, None] * (proj * first[group][:, None] - second[group])
    hessvec = jnp.dot(resid.T, covars, precision=lax.Precision.HIGHEST)
    return hessvec / total
```

```python
import functools

import jax
import jax.numpy as jnp
from jax import lax
from jax.experimental import pallas as pl
from jax.experimental.pallas import tpu as pltpu
from jax.sharding import PartitionSpec as P

G_SH = 256
BF16 = jnp.bfloat16
F32 = jnp.float32


def split3(x):
    hi = x.astype(BF16).astype(F32)
    rest = x - hi
    mid = rest.astype(BF16).astype(F32)
    return hi, mid, rest - mid


def stack3(x):
    hi, mid, low = split3(x)
    return jnp.concatenate([hi, mid, low, jnp.zeros_like(x)], axis=0).astype(BF16)


def unstack3(y):
    return (y[16:24] + y[8:16]) + y[0:8]


def pad8(rows):
    width = rows[0].shape[1]
    used = sum(r.shape[0] for r in rows)
    return jnp.concatenate(list(rows) + [jnp.zeros((8 - used, width), F32)], axis=0)


def first_pass(
    chunk, covars, events, group, counts, shard, beta, vecs,
    lin, died, valid, member, high, low,
    buf, beta_v, vecs_v, group_v, events_v, count_s, shard_s, sems, small,
):
    rows = covars.shape[0]
    steps = rows // chunk
    copies = [
        pltpu.make_async_copy(group, group_v, small.at[0]),
        pltpu.make_async_copy(beta, beta_v, small.at[1]),
        pltpu.make_async_copy(vecs, vecs_v, small.at[2]),
        pltpu.make_async_copy(events, events_v, small.at[3]),
        pltpu.make_async_copy(counts, count_s, small.at[4]),
        pltpu.make_async_copy(shard, shard_s, small.at[5]),
    ]
    for copy in copies:
        copy.start()

    def piece(step):
        at = pl.ds(pl.multiple_of(step * chunk, chunk), chunk)
        return pltpu.make_async_copy(covars.at[at], buf.at[at], sems.at[step])

    for step in range(steps):
        piece(step).start()
    for copy in copies:
        copy.wait()
    index = lax.broadcasted_iota(jnp.int32, (1, rows), 1)
    ok = index < count_s[0]
    valid[...] = jnp.where(ok, 1.0, 0.0)
    died[...] = jnp.where(ok, events_v[...].astype(F32), 0.0)
    coeffs = stack3(pad8([beta_v[...], vecs_v[...]]))
    base = shard_s[0] * G_SH

    def body(step, carry):
        at = pl.ds(pl.multiple_of(step * chunk, chunk), chunk)
        labels = group_v[:, at] - base
        groups = lax.broadcasted_iota(jnp.int32, (G_SH, chunk), 0)
        member[:, at] = jnp.where(groups == labels, 1.0, 0.0).astype(BF16)
        piece(step).wait()
        full = buf[at, :]
        hi = full.astype(BF16)
        lo = (full - hi.astype(F32)).astype(BF16)
        high[at, :] = hi
        low[at, :] = lo
        dims = (((1,), (1,)), ((), ()))
        out = lax.dot_general(coeffs, hi, dims, preferred_element_type=F32)
        out += lax.dot_general(coeffs, lo, dims, preferred_element_type=F32)
        lin[:, at] = unstack3(out)[0:3]
        return carry

    lax.fori_loop(0, steps, body, 0)


def tally(mine, other, valid, died, member, stats, weighted):
    total = mine[...] + other[...]
    weight = jnp.where(valid[...] > 0.0, jnp.exp(total[0:1]), 0.0)
    proj = total[1:3]
    weighted[0:1] = weight
    weighted[1:3] = proj
    rows = pad8([weight, weight * proj, died[...]])
    out = lax.dot_general(
        stack3(rows), member[...], (((1,), (1,)), ((), ())), preferred_element_type=F32
    )
    sums = unstack3(out)[0:4]
    for slot in range(stats.shape[0]):
        stats[slot] = sums


def second_pass(shards, scale, shard, stats, weighted, member, high, low, out):
    me = shard[0]
    peers = stats.shape[0]
    each = peers // shards
    per_shard = []
    for s in range(shards):
        acc = stats[s * each]
        for p in range(1, each):
            acc = acc + stats[s * each + p]
        per_shard.append(acc)
    width = per_shard[0].shape[1]
    row = lax.broadcasted_iota(jnp.int32, (width, width), 0)
    col = lax.broadcasted_iota(jnp.int32, (width, width), 1)
    suffix = jnp.where(row >= col, 1.0, 0.0).astype(BF16)
    prefix = jnp.where(row <= col, 1.0, 0.0).astype(BF16)

    tail = jnp.zeros((4, 1), F32)
    tails = [None] * shards
    for s in reversed(range(shards)):
        tails[s] = tail
        tail = tail + jnp.sum(per_shard[s], axis=1, keepdims=True)

    def ratios_of(s):
        mat = stack3(pad8([per_shard[s]]))
        risk = unstack3(jnp.dot(mat, suffix, preferred_element_type=F32))[0:4] + tails[s]
        died_grp = per_shard[s][3:4]
        risk0 = risk[0:1]
        return pad8([died_grp / risk0, died_grp * risk[1:3] / (risk0 * risk0)])

    chosen = jnp.zeros((8, width), F32)
    head = jnp.zeros((8, 1), F32)
    for s in range(shards):
        value = ratios_of(s)
        chosen = jnp.where(me == s, value, chosen)
        head = head + jnp.where(me > s, jnp.sum(value, axis=1, keepdims=True), 0.0)
    cumulative = unstack3(jnp.dot(stack3(chosen), prefix, preferred_element_type=F32)) + head
    looked = unstack3(jnp.dot(stack3(cumulative), member[...], preferred_element_type=F32))
    weight = weighted[0:1]
    proj = weighted[1:3]
    resid = weight * (proj * looked[0:1] - looked[1:3])
    lhs = stack3(pad8([resid]))
    prod = jnp.dot(lhs, high[...], preferred_element_type=F32)
    prod += jnp.dot(lhs, low[...], preferred_element_type=F32)
    prod = unstack3(prod)[0:2] * scale
    for slot in range(out.shape[0]):
        out[slot] = prod


def per_device(covars, events, group, counts, beta, vecs):
    rows, cols = covars.shape
    shards = lax.axis_size("tm")
    peers = shards * lax.axis_size("loan")
    records = rows * peers
    chunk = min(512, rows)
    shard = lax.axis_index("tm").astype(jnp.int32)[None]
    hbm = pl.BlockSpec(memory_space=pltpu.HBM)
    vmem = pl.BlockSpec(memory_space=pltpu.VMEM)
    smem = pl.BlockSpec(memory_space=pltpu.SMEM)

    def arr(shape, dtype=F32):
        return jax.ShapeDtypeStruct(shape, dtype)

    def kept(shape, dtype=F32):
        return pltpu.VMEM(shape, dtype)

    lin, died, valid, member, high, low = pl.pallas_call(
        functools.partial(first_pass, chunk),
        out_shape=(
            arr((3, rows)), arr((1, rows)), arr((1, rows)),
            kept((G_SH, rows), BF16), kept((rows, cols), BF16), kept((rows, cols), BF16),
        ),
        in_specs=[hbm] * 7,
        out_specs=(vmem,) * 6,
        scratch_shapes=[
            pltpu.VMEM((rows, cols), F32),
            pltpu.VMEM((1, cols), F32),
            pltpu.VMEM((2, cols), F32),
            pltpu.VMEM((1, rows), jnp.int32),
            pltpu.VMEM((1, rows), jnp.int32),
            pltpu.SMEM((1,), jnp.int32),
            pltpu.SMEM((1,), jnp.int32),
            pltpu.SemaphoreType.DMA((rows // chunk,)),
            pltpu.SemaphoreType.DMA((6,)),
        ],
        compiler_params=pltpu.CompilerParams(vmem_limit_bytes=24 << 20),
        name="first_pass",
    )(covars, events[None], group[None], counts, shard, beta[None], vecs)

    pairs = [(i, i ^ 1) for i in range(2)]
    other = lax.ppermute(lin, "cov", pairs)

    stats, weighted = pl.pallas_call(
        tally,
        out_shape=(arr((peers, 4, G_SH)), arr((3, rows))),
        in_specs=[vmem] * 5,
        out_specs=(vmem,) * 2,
        compiler_params=pltpu.CompilerParams(vmem_limit_bytes=16 << 20),
        name="tally",
    )(lin, other, valid, died, member)

    everyone = lax.all_to_all(stats, ("tm", "loan"), 0, 0)

    parts = pl.pallas_call(
        functools.partial(second_pass, shards, 1.0 / records),
        out_shape=arr((peers, 2, cols)),
        in_specs=[smem] + [vmem] * 5,
        out_specs=vmem,
        compiler_params=pltpu.CompilerParams(vmem_limit_bytes=16 << 20),
        name="second_pass",
    )(shard, everyone, weighted, member, high, low)

    return jnp.sum(lax.all_to_all(parts, ("tm", "loan"), 0, 0), axis=0)


def solution(mesh):
    return jax.shard_map(
        per_device,
        mesh=mesh,
        in_specs=(
            P(("tm", "loan"), "cov"),
            P(("tm", "loan")),
            P(("tm", "loan")),
            P(("tm", "loan")),
            P("cov"),
            P(None, "cov"),
        ),
        out_specs=P(None, "cov"),
        check_vma=False,
    )
```

```python
import functools

import jax
import jax.numpy as jnp
from jax import lax
from jax.experimental import pallas as pl
from jax.experimental.pallas import tpu as pltpu
from jax.sharding import PartitionSpec as P

G_SH = 256
BF16 = jnp.bfloat16
F32 = jnp.float32


def split3(x):
    hi = x.astype(BF16).astype(F32)
    rest = x - hi
    mid = rest.astype(BF16).astype(F32)
    return hi, mid, rest - mid


def stack3(x):
    hi, mid, low = split3(x)
    return jnp.concatenate([hi, mid, low, jnp.zeros_like(x)], axis=0).astype(BF16)


def unstack3(y):
    return (y[16:24] + y[8:16]) + y[0:8]


def pad8(rows):
    width = rows[0].shape[1]
    used = sum(r.shape[0] for r in rows)
    return jnp.concatenate(list(rows) + [jnp.zeros((8 - used, width), F32)], axis=0)


def first_pass(
    chunk, covars, events, group, counts, shard, beta, vecs,
    lin, died, valid, member, high, low,
    buf, beta_v, vecs_v, group_v, events_v, sems, small,
):
    rows = covars.shape[0]
    steps = rows // chunk
    copies = [
        pltpu.make_async_copy(group, group_v, small.at[0]),
        pltpu.make_async_copy(beta, beta_v, small.at[1]),
        pltpu.make_async_copy(vecs, vecs_v, small.at[2]),
        pltpu.make_async_copy(events, events_v, small.at[3]),
    ]
    for copy in copies:
        copy.start()

    def piece(step):
        at = pl.ds(pl.multiple_of(step * chunk, chunk), chunk)
        return pltpu.make_async_copy(covars.at[at], buf.at[at], sems.at[step])

    for step in range(steps):
        piece(step).start()
    for copy in copies:
        copy.wait()
    index = lax.broadcasted_iota(jnp.int32, (1, rows), 1)
    ok = index < counts[0]
    valid[...] = jnp.where(ok, 1.0, 0.0)
    died[...] = jnp.where(ok, events_v[...].astype(F32), 0.0)
    coeffs = stack3(pad8([beta_v[...], vecs_v[...]]))
    base = shard[0] * G_SH

    def body(step, carry):
        at = pl.ds(pl.multiple_of(step * chunk, chunk), chunk)
        labels = group_v[:, at] - base
        groups = lax.broadcasted_iota(jnp.int32, (G_SH, chunk), 0)
        member[:, at] = jnp.where(groups == labels, 1.0, 0.0).astype(BF16)
        piece(step).wait()
        full = buf[at, :]
        hi = full.astype(BF16)
        lo = (full - hi.astype(F32)).astype(BF16)
        high[at, :] = hi
        low[at, :] = lo
        dims = (((1,), (1,)), ((), ()))
        out = lax.dot_general(coeffs, hi, dims, preferred_element_type=F32)
        out += lax.dot_general(coeffs, lo, dims, preferred_element_type=F32)
        lin[:, at] = unstack3(out)[0:3]
        return carry

    lax.fori_loop(0, steps, body, 0)


def tally(mine, other, valid, died, member, stats, weighted):
    total = mine[...] + other[...]
    weight = jnp.where(valid[...] > 0.0, jnp.exp(total[0:1]), 0.0)
    proj = total[1:3]
    weighted[0:1] = weight
    weighted[1:3] = proj
    rows = pad8([weight, weight * proj, died[...]])
    out = lax.dot_general(
        stack3(rows), member[...], (((1,), (1,)), ((), ())), preferred_element_type=F32
    )
    sums = unstack3(out)[0:4]
    for slot in range(stats.shape[0]):
        stats[slot] = sums


def second_pass(shards, scale, shard, stats, weighted, member, high, low, out):
    me = shard[0]
    peers = stats.shape[0]
    each = peers // shards
    per_shard = []
    for s in range(shards):
        acc = stats[s * each]
        for p in range(1, each):
            acc = acc + stats[s * each + p]
        per_shard.append(acc)
    width = per_shard[0].shape[1]
    row = lax.broadcasted_iota(jnp.int32, (width, width), 0)
    col = lax.broadcasted_iota(jnp.int32, (width, width), 1)
    suffix = jnp.where(row >= col, 1.0, 0.0).astype(BF16)
    prefix = jnp.where(row <= col, 1.0, 0.0).astype(BF16)

    tail = jnp.zeros((4, 1), F32)
    tails = [None] * shards
    for s in reversed(range(shards)):
        tails[s] = tail
        tail = tail + jnp.sum(per_shard[s], axis=1, keepdims=True)

    def ratios_of(s):
        mat = stack3(pad8([per_shard[s]]))
        risk = unstack3(jnp.dot(mat, suffix, preferred_element_type=F32))[0:4] + tails[s]
        died_grp = per_shard[s][3:4]
        risk0 = risk[0:1]
        return pad8([died_grp / risk0, died_grp * risk[1:3] / (risk0 * risk0)])

    chosen = jnp.zeros((8, width), F32)
    head = jnp.zeros((8, 1), F32)
    for s in range(shards):
        value = ratios_of(s)
        chosen = jnp.where(me == s, value, chosen)
        head = head + jnp.where(me > s, jnp.sum(value, axis=1, keepdims=True), 0.0)
    cumulative = unstack3(jnp.dot(stack3(chosen), prefix, preferred_element_type=F32)) + head
    looked = unstack3(jnp.dot(stack3(cumulative), member[...], preferred_element_type=F32))
    weight = weighted[0:1]
    proj = weighted[1:3]
    resid = weight * (proj * looked[0:1] - looked[1:3])
    lhs = stack3(pad8([resid]))
    prod = jnp.dot(lhs, high[...], preferred_element_type=F32)
    prod += jnp.dot(lhs, low[...], preferred_element_type=F32)
    prod = unstack3(prod)[0:2] * scale
    for slot in range(out.shape[0]):
        out[slot] = prod


def per_device(covars, events, group, counts, beta, vecs):
    rows, cols = covars.shape
    shards = lax.axis_size("tm")
    peers = shards * lax.axis_size("loan")
    records = rows * peers
    chunk = min(512, rows)
    shard = lax.axis_index("tm").astype(jnp.int32)[None]
    hbm = pl.BlockSpec(memory_space=pltpu.HBM)
    vmem = pl.BlockSpec(memory_space=pltpu.VMEM)
    smem = pl.BlockSpec(memory_space=pltpu.SMEM)

    def arr(shape, dtype=F32):
        return jax.ShapeDtypeStruct(shape, dtype)

    def kept(shape, dtype=F32):
        return pltpu.VMEM(shape, dtype)

    lin, died, valid, member, high, low = pl.pallas_call(
        functools.partial(first_pass, chunk),
        out_shape=(
            arr((3, rows)), arr((1, rows)), arr((1, rows)),
            kept((G_SH, rows), BF16), kept((rows, cols), BF16), kept((rows, cols), BF16),
        ),
        in_specs=[hbm] * 3 + [smem] * 2 + [hbm] * 2,
        out_specs=(vmem,) * 6,
        scratch_shapes=[
            pltpu.VMEM((rows, cols), F32),
            pltpu.VMEM((1, cols), F32),
            pltpu.VMEM((2, cols), F32),
            pltpu.VMEM((1, rows), jnp.int32),
            pltpu.VMEM((1, rows), jnp.int32),
            pltpu.SemaphoreType.DMA((rows // chunk,)),
            pltpu.SemaphoreType.DMA((4,)),
        ],
        compiler_params=pltpu.CompilerParams(vmem_limit_bytes=24 << 20),
        name="first_pass",
    )(
        *(
            pltpu.with_memory_space_constraint(x, pltpu.HBM)
            for x in (covars, events[None], group[None])
        ),
        counts,
        shard,
        *(pltpu.with_memory_space_constraint(x, pltpu.HBM) for x in (beta[None], vecs)),
    )

    pairs = [(i, i ^ 1) for i in range(2)]
    other = lax.ppermute(lin, "cov", pairs)

    stats, weighted = pl.pallas_call(
        tally,
        out_shape=(arr((peers, 4, G_SH)), arr((3, rows))),
        in_specs=[vmem] * 5,
        out_specs=(vmem,) * 2,
        compiler_params=pltpu.CompilerParams(vmem_limit_bytes=16 << 20),
        name="tally",
    )(lin, other, valid, died, member)

    everyone = lax.all_to_all(stats, ("tm", "loan"), 0, 0)

    parts = pl.pallas_call(
        functools.partial(second_pass, shards, 1.0 / records),
        out_shape=arr((peers, 2, cols)),
        in_specs=[smem] + [vmem] * 5,
        out_specs=vmem,
        compiler_params=pltpu.CompilerParams(vmem_limit_bytes=16 << 20),
        name="second_pass",
    )(shard, everyone, weighted, member, high, low)

    return jnp.sum(lax.all_to_all(parts, ("tm", "loan"), 0, 0), axis=0)


def solution(mesh):
    return jax.shard_map(
        per_device,
        mesh=mesh,
        in_specs=(
            P(("tm", "loan"), "cov"),
            P(("tm", "loan")),
            P(("tm", "loan")),
            P(("tm", "loan")),
            P("cov"),
            P(None, "cov"),
        ),
        out_specs=P(None, "cov"),
        check_vma=False,
    )
```

```python
import functools

import jax
import jax.numpy as jnp
from jax import lax
from jax.experimental import pallas as pl
from jax.experimental.pallas import tpu as pltpu
from jax.sharding import PartitionSpec as P

G_SH = 256
BF16 = jnp.bfloat16
F32 = jnp.float32


def split3(x):
    hi = x.astype(BF16).astype(F32)
    rest = x - hi
    mid = rest.astype(BF16).astype(F32)
    return hi, mid, rest - mid


def stack3(x):
    hi, mid, low = split3(x)
    return jnp.concatenate([hi, mid, low, jnp.zeros_like(x)], axis=0).astype(BF16)


def unstack3(y):
    return (y[16:24] + y[8:16]) + y[0:8]


def pad8(rows):
    width = rows[0].shape[1]
    used = sum(r.shape[0] for r in rows)
    return jnp.concatenate(list(rows) + [jnp.zeros((8 - used, width), F32)], axis=0)


def first_pass(
    chunk, covars, events, group, counts, shard, beta, vecs,
    lin, died, valid, member, high, low,
    buf, beta_v, vecs_v, group_v, events_v, sems, small,
):
    rows = covars.shape[0]
    steps = rows // chunk
    copies = [
        pltpu.make_async_copy(group, group_v, small.at[0]),
        pltpu.make_async_copy(beta, beta_v, small.at[1]),
        pltpu.make_async_copy(vecs, vecs_v, small.at[2]),
        pltpu.make_async_copy(events, events_v, small.at[3]),
    ]
    for copy in copies:
        copy.start()

    def piece(step):
        at = pl.ds(pl.multiple_of(step * chunk, chunk), chunk)
        return pltpu.make_async_copy(covars.at[at], buf.at[at], sems.at[step])

    piece(0).start()
    if steps > 1:
        piece(1).start()
    for copy in copies:
        copy.wait()
    index = lax.broadcasted_iota(jnp.int32, (1, rows), 1)
    ok = index < counts[0]
    valid[...] = jnp.where(ok, 1.0, 0.0)
    died[...] = jnp.where(ok, events_v[...].astype(F32), 0.0)
    coeffs = stack3(pad8([beta_v[...], vecs_v[...]]))
    base = shard[0] * G_SH
    part = min(512, chunk)

    def mark(step, carry):
        at = pl.ds(pl.multiple_of(step * part, part), part)
        labels = (group_v[:, at] - base).astype(F32).astype(BF16)
        groups = lax.broadcasted_iota(jnp.int32, (G_SH, part), 0).astype(F32).astype(BF16)
        member[:, at] = jnp.where(groups == labels, jnp.ones((), BF16), jnp.zeros((), BF16))
        return carry

    lax.fori_loop(0, rows // part, mark, 0)
    if steps > 2:
        piece(2).start()

    def body(step, carry):
        at = pl.ds(pl.multiple_of(step * chunk, chunk), chunk)
        piece(step).wait()

        @pl.when(step + 3 < steps)
        def _():
            piece(step + 3).start()

        full = buf[at, :]
        hi = full.astype(BF16)
        lo = (full - hi.astype(F32)).astype(BF16)
        high[at, :] = hi
        low[at, :] = lo
        dims = (((1,), (1,)), ((), ()))
        out = lax.dot_general(coeffs, hi, dims, preferred_element_type=F32)
        out += lax.dot_general(coeffs, lo, dims, preferred_element_type=F32)
        lin[:, at] = unstack3(out)[0:3]
        return carry

    lax.fori_loop(0, steps, body, 0)


def tally(mine, other, valid, died, member, stats, weighted):
    total = mine[...] + other[...]
    weight = jnp.where(valid[...] > 0.0, jnp.exp(total[0:1]), 0.0)
    proj = total[1:3]
    weighted[0:1] = weight
    weighted[1:3] = proj
    rows = pad8([weight, weight * proj, died[...]])
    out = lax.dot_general(
        stack3(rows), member[...], (((1,), (1,)), ((), ())), preferred_element_type=F32
    )
    sums = unstack3(out)[0:4]
    for slot in range(stats.shape[0]):
        stats[slot] = sums


def second_pass(shards, scale, shard, stats, weighted, member, high, low, out):
    me = shard[0]
    peers = stats.shape[0]
    each = peers // shards
    per_shard = []
    for s in range(shards):
        acc = stats[s * each]
        for p in range(1, each):
            acc = acc + stats[s * each + p]
        per_shard.append(acc)
    width = per_shard[0].shape[1]
    row = lax.broadcasted_iota(jnp.int32, (width, width), 0)
    col = lax.broadcasted_iota(jnp.int32, (width, width), 1)
    suffix = jnp.where(row >= col, 1.0, 0.0).astype(BF16)
    prefix = jnp.where(row <= col, 1.0, 0.0).astype(BF16)

    tail = jnp.zeros((4, 1), F32)
    tails = [None] * shards
    for s in reversed(range(shards)):
        tails[s] = tail
        tail = tail + jnp.sum(per_shard[s], axis=1, keepdims=True)

    def ratios_of(s):
        mat = stack3(pad8([per_shard[s]]))
        risk = unstack3(jnp.dot(mat, suffix, preferred_element_type=F32))[0:4] + tails[s]
        died_grp = per_shard[s][3:4]
        risk0 = risk[0:1]
        return pad8([died_grp / risk0, died_grp * risk[1:3] / (risk0 * risk0)])

    chosen = jnp.zeros((8, width), F32)
    head = jnp.zeros((8, 1), F32)
    for s in range(shards):
        value = ratios_of(s)
        chosen = jnp.where(me == s, value, chosen)
        head = head + jnp.where(me > s, jnp.sum(value, axis=1, keepdims=True), 0.0)
    cumulative = unstack3(jnp.dot(stack3(chosen), prefix, preferred_element_type=F32)) + head
    looked = unstack3(jnp.dot(stack3(cumulative), member[...], preferred_element_type=F32))
    weight = weighted[0:1]
    proj = weighted[1:3]
    resid = weight * (proj * looked[0:1] - looked[1:3])
    lhs = stack3(pad8([resid]))
    prod = jnp.dot(lhs, high[...], preferred_element_type=F32)
    prod += jnp.dot(lhs, low[...], preferred_element_type=F32)
    prod = unstack3(prod)[0:2] * scale
    for slot in range(out.shape[0]):
        out[slot] = prod


def per_device(covars, events, group, counts, beta, vecs):
    rows, cols = covars.shape
    shards = lax.axis_size("tm")
    peers = shards * lax.axis_size("loan")
    records = rows * peers
    chunk = min(1024, rows)
    shard = lax.axis_index("tm").astype(jnp.int32)[None]
    hbm = pl.BlockSpec(memory_space=pltpu.HBM)
    vmem = pl.BlockSpec(memory_space=pltpu.VMEM)
    smem = pl.BlockSpec(memory_space=pltpu.SMEM)

    def arr(shape, dtype=F32):
        return jax.ShapeDtypeStruct(shape, dtype)

    def kept(shape, dtype=F32):
        return pltpu.VMEM(shape, dtype)

    lin, died, valid, member, high, low = pl.pallas_call(
        functools.partial(first_pass, chunk),
        out_shape=(
            arr((3, rows)), arr((1, rows)), arr((1, rows)),
            kept((G_SH, rows), BF16), kept((rows, cols), BF16), kept((rows, cols), BF16),
        ),
        in_specs=[hbm] * 3 + [smem] * 2 + [hbm] * 2,
        out_specs=(vmem,) * 6,
        scratch_shapes=[
            pltpu.VMEM((rows, cols), F32),
            pltpu.VMEM((1, cols), F32),
            pltpu.VMEM((2, cols), F32),
            pltpu.VMEM((1, rows), jnp.int32),
            pltpu.VMEM((1, rows), jnp.int32),
            pltpu.SemaphoreType.DMA((rows // chunk,)),
            pltpu.SemaphoreType.DMA((4,)),
        ],
        compiler_params=pltpu.CompilerParams(vmem_limit_bytes=24 << 20),
        name="first_pass",
    )(
        *(
            pltpu.with_memory_space_constraint(x, pltpu.HBM)
            for x in (covars, events[None], group[None])
        ),
        counts,
        shard,
        *(pltpu.with_memory_space_constraint(x, pltpu.HBM) for x in (beta[None], vecs)),
    )

    pairs = [(i, i ^ 1) for i in range(2)]
    other = lax.ppermute(lin, "cov", pairs)

    stats, weighted = pl.pallas_call(
        tally,
        out_shape=(arr((peers, 4, G_SH)), arr((3, rows))),
        in_specs=[vmem] * 5,
        out_specs=(vmem,) * 2,
        compiler_params=pltpu.CompilerParams(vmem_limit_bytes=16 << 20),
        name="tally",
    )(lin, other, valid, died, member)

    everyone = lax.all_to_all(stats, ("tm", "loan"), 0, 0)

    parts = pl.pallas_call(
        functools.partial(second_pass, shards, 1.0 / records),
        out_shape=arr((peers, 2, cols)),
        in_specs=[smem] + [vmem] * 5,
        out_specs=vmem,
        compiler_params=pltpu.CompilerParams(vmem_limit_bytes=16 << 20),
        name="second_pass",
    )(shard, everyone, weighted, member, high, low)

    return jnp.sum(lax.all_to_all(parts, ("tm", "loan"), 0, 0), axis=0)


def solution(mesh):
    return jax.shard_map(
        per_device,
        mesh=mesh,
        in_specs=(
            P(("tm", "loan"), "cov"),
            P(("tm", "loan")),
            P(("tm", "loan")),
            P(("tm", "loan")),
            P("cov"),
            P(None, "cov"),
        ),
        out_specs=P(None, "cov"),
        check_vma=False,
    )
```

```python
import functools

import jax
import jax.numpy as jnp
from jax import lax
from jax.experimental import pallas as pl
from jax.experimental.pallas import tpu as pltpu
from jax.sharding import PartitionSpec as P

G_SH = 256
BF16 = jnp.bfloat16
F32 = jnp.float32


def split3(x):
    hi = x.astype(BF16).astype(F32)
    rest = x - hi
    mid = rest.astype(BF16).astype(F32)
    return hi, mid, rest - mid


def stack3(x):
    hi, mid, low = split3(x)
    return jnp.concatenate([hi, mid, low, jnp.zeros_like(x)], axis=0).astype(BF16)


def unstack3(y):
    return (y[16:24] + y[8:16]) + y[0:8]


def pad8(rows):
    width = rows[0].shape[1]
    used = sum(r.shape[0] for r in rows)
    return jnp.concatenate(list(rows) + [jnp.zeros((8 - used, width), F32)], axis=0)


def first_pass(
    chunk, covars, events, group, counts, shard, beta, vecs,
    lin, died, valid, reach, high, low,
    buf, beta_v, vecs_v, group_v, events_v, sems, small,
):
    rows = covars.shape[0]
    steps = rows // chunk
    copies = [
        pltpu.make_async_copy(group, group_v, small.at[0]),
        pltpu.make_async_copy(beta, beta_v, small.at[1]),
        pltpu.make_async_copy(vecs, vecs_v, small.at[2]),
        pltpu.make_async_copy(events, events_v, small.at[3]),
    ]
    for copy in copies:
        copy.start()

    def piece(step):
        at = pl.ds(pl.multiple_of(step * chunk, chunk), chunk)
        return pltpu.make_async_copy(covars.at[at], buf.at[at], sems.at[step])

    piece(0).start()
    if steps > 1:
        piece(1).start()
    for copy in copies:
        copy.wait()
    index = lax.broadcasted_iota(jnp.int32, (1, rows), 1)
    ok = index < counts[0]
    valid[...] = jnp.where(ok, 1.0, 0.0)
    died[...] = jnp.where(ok, events_v[...].astype(F32), 0.0)
    coeffs = stack3(pad8([beta_v[...], vecs_v[...]]))
    base = shard[0] * G_SH
    part = min(512, chunk)

    def mark(step, carry):
        at = pl.ds(pl.multiple_of(step * part, part), part)
        labels = (group_v[:, at] - base).astype(F32).astype(BF16)
        groups = lax.broadcasted_iota(jnp.int32, (G_SH, part), 0).astype(F32).astype(BF16)
        reach[:, at] = jnp.where(groups <= labels, jnp.ones((), BF16), jnp.zeros((), BF16))
        return carry

    lax.fori_loop(0, rows // part, mark, 0)
    if steps > 2:
        piece(2).start()

    def body(step, carry):
        at = pl.ds(pl.multiple_of(step * chunk, chunk), chunk)
        piece(step).wait()

        @pl.when(step + 3 < steps)
        def _():
            piece(step + 3).start()

        full = buf[at, :]
        hi = full.astype(BF16)
        lo = (full - hi.astype(F32)).astype(BF16)
        high[at, :] = hi
        low[at, :] = lo
        dims = (((1,), (1,)), ((), ()))
        out = lax.dot_general(coeffs, hi, dims, preferred_element_type=F32)
        out += lax.dot_general(coeffs, lo, dims, preferred_element_type=F32)
        lin[:, at] = unstack3(out)[0:3]
        return carry

    lax.fori_loop(0, steps, body, 0)


def tally(mine, other, valid, died, reach, stats, weighted):
    total = mine[...] + other[...]
    weight = jnp.where(valid[...] > 0.0, jnp.exp(total[0:1]), 0.0)
    proj = total[1:3]
    weighted[0:1] = weight
    weighted[1:3] = proj
    rows = pad8([weight, weight * proj, died[...]])
    out = lax.dot_general(
        stack3(rows), reach[...], (((1,), (1,)), ((), ())), preferred_element_type=F32
    )
    sums = unstack3(out)[0:4]
    for slot in range(stats.shape[0]):
        stats[slot] = sums


def second_pass(shards, scale, shard, stats, weighted, reach, high, low, out):
    me = shard[0]
    peers = stats.shape[0]
    each = peers // shards
    per_shard = []
    for s in range(shards):
        acc = stats[s * each]
        for p in range(1, each):
            acc = acc + stats[s * each + p]
        per_shard.append(acc)
    width = per_shard[0].shape[1]
    lane = lax.broadcasted_iota(jnp.int32, (1, width), 1)

    tail = jnp.zeros((4, 1), F32)
    tails = [None] * shards
    for s in reversed(range(shards)):
        tails[s] = tail
        tail = tail + per_shard[s][:, 0:1]

    def ratios_of(s):
        risk = per_shard[s] + tails[s]
        late = per_shard[s][3:4]
        died_grp = late - jnp.where(lane == width - 1, 0.0, pltpu.roll(late, width - 1, 1))
        risk0 = risk[0:1]
        return pad8([died_grp / risk0, died_grp * risk[1:3] / (risk0 * risk0)])

    chosen = jnp.zeros((8, width), F32)
    head = jnp.zeros((8, 1), F32)
    for s in range(shards):
        value = ratios_of(s)
        chosen = jnp.where(me == s, value, chosen)
        head = head + jnp.where(me > s, jnp.sum(value, axis=1, keepdims=True), 0.0)
    looked = unstack3(jnp.dot(stack3(chosen), reach[...], preferred_element_type=F32)) + head
    weight = weighted[0:1]
    proj = weighted[1:3]
    resid = weight * (proj * looked[0:1] - looked[1:3])
    lhs = stack3(pad8([resid]))
    prod = jnp.dot(lhs, high[...], preferred_element_type=F32)
    prod += jnp.dot(lhs, low[...], preferred_element_type=F32)
    prod = unstack3(prod)[0:2] * scale
    for slot in range(out.shape[0]):
        out[slot] = prod


def per_device(covars, events, group, counts, beta, vecs):
    rows, cols = covars.shape
    shards = lax.axis_size("tm")
    peers = shards * lax.axis_size("loan")
    records = rows * peers
    chunk = min(1024, rows)
    shard = lax.axis_index("tm").astype(jnp.int32)[None]
    hbm = pl.BlockSpec(memory_space=pltpu.HBM)
    vmem = pl.BlockSpec(memory_space=pltpu.VMEM)
    smem = pl.BlockSpec(memory_space=pltpu.SMEM)

    def arr(shape, dtype=F32):
        return jax.ShapeDtypeStruct(shape, dtype)

    def kept(shape, dtype=F32):
        return pltpu.VMEM(shape, dtype)

    lin, died, valid, reach, high, low = pl.pallas_call(
        functools.partial(first_pass, chunk),
        out_shape=(
            arr((3, rows)), arr((1, rows)), arr((1, rows)),
            kept((G_SH, rows), BF16), kept((rows, cols), BF16), kept((rows, cols), BF16),
        ),
        in_specs=[hbm] * 3 + [smem] * 2 + [hbm] * 2,
        out_specs=(vmem,) * 6,
        scratch_shapes=[
            pltpu.VMEM((rows, cols), F32),
            pltpu.VMEM((1, cols), F32),
            pltpu.VMEM((2, cols), F32),
            pltpu.VMEM((1, rows), jnp.int32),
            pltpu.VMEM((1, rows), jnp.int32),
            pltpu.SemaphoreType.DMA((rows // chunk,)),
            pltpu.SemaphoreType.DMA((4,)),
        ],
        compiler_params=pltpu.CompilerParams(vmem_limit_bytes=24 << 20),
        name="first_pass",
    )(
        *(
            pltpu.with_memory_space_constraint(x, pltpu.HBM)
            for x in (covars, events[None], group[None])
        ),
        counts,
        shard,
        *(pltpu.with_memory_space_constraint(x, pltpu.HBM) for x in (beta[None], vecs)),
    )

    pairs = [(i, i ^ 1) for i in range(2)]
    other = lax.ppermute(lin, "cov", pairs)

    stats, weighted = pl.pallas_call(
        tally,
        out_shape=(arr((peers, 4, G_SH)), arr((3, rows))),
        in_specs=[vmem] * 5,
        out_specs=(vmem,) * 2,
        compiler_params=pltpu.CompilerParams(vmem_limit_bytes=16 << 20),
        name="tally",
    )(lin, other, valid, died, reach)

    everyone = lax.all_to_all(stats, ("tm", "loan"), 0, 0)

    parts = pl.pallas_call(
        functools.partial(second_pass, shards, 1.0 / records),
        out_shape=arr((peers, 2, cols)),
        in_specs=[smem] + [vmem] * 5,
        out_specs=vmem,
        compiler_params=pltpu.CompilerParams(vmem_limit_bytes=16 << 20),
        name="second_pass",
    )(shard, everyone, weighted, reach, high, low)

    return jnp.sum(lax.all_to_all(parts, ("tm", "loan"), 0, 0), axis=0)


def solution(mesh):
    return jax.shard_map(
        per_device,
        mesh=mesh,
        in_specs=(
            P(("tm", "loan"), "cov"),
            P(("tm", "loan")),
            P(("tm", "loan")),
            P(("tm", "loan")),
            P("cov"),
            P(None, "cov"),
        ),
        out_specs=P(None, "cov"),
        check_vma=False,
    )
```

```python
import functools

import jax
import jax.numpy as jnp
from jax import lax
from jax.experimental import pallas as pl
from jax.experimental.pallas import tpu as pltpu
from jax.sharding import PartitionSpec as P

G_SH = 256
LANES = 128
BF16 = jnp.bfloat16
F32 = jnp.float32


def split3(x):
    hi = x.astype(BF16).astype(F32)
    rest = x - hi
    mid = rest.astype(BF16).astype(F32)
    return hi, mid, rest - mid


def stack3(x):
    used, width = x.shape
    rest = jnp.zeros((16 - 3 * used, width), F32)
    return jnp.concatenate([*split3(x), rest], axis=0).astype(BF16)


def unstack3(y, used):
    return (y[2 * used : 3 * used] + y[used : 2 * used]) + y[0:used]


def first_pass(
    chunk, covars, events, group, counts, shard, beta, vecs,
    lin, died, valid, reach, high, low,
    buf, beta_v, vecs_v, group_v, events_v, sems, small,
):
    rows = covars.shape[0]
    steps = rows // chunk
    copies = [
        pltpu.make_async_copy(group, group_v, small.at[0]),
        pltpu.make_async_copy(beta, beta_v, small.at[1]),
        pltpu.make_async_copy(vecs, vecs_v, small.at[2]),
        pltpu.make_async_copy(events, events_v, small.at[3]),
    ]
    for copy in copies:
        copy.start()

    def piece(step):
        at = pl.ds(pl.multiple_of(step * chunk, chunk), chunk)
        return pltpu.make_async_copy(covars.at[at], buf.at[at], sems.at[step])

    piece(0).start()
    if steps > 1:
        piece(1).start()
    for copy in copies:
        copy.wait()
    dense = (rows // LANES, LANES)
    index = lax.broadcasted_iota(jnp.int32, dense, 0) * LANES
    ok = index + lax.broadcasted_iota(jnp.int32, dense, 1) < counts[0]
    valid[...] = jnp.where(ok, 1.0, 0.0)
    died[...] = jnp.where(ok, events_v[...].astype(F32), 0.0)
    coeffs = stack3(jnp.concatenate([beta_v[...], vecs_v[...]], axis=0))
    base = shard[0] * G_SH
    part = min(512, chunk)

    def mark(step, carry):
        at = pl.ds(pl.multiple_of(step * part, part), part)
        labels = (group_v[:, at] - base).astype(F32).astype(BF16)
        groups = lax.broadcasted_iota(jnp.int32, (G_SH, part), 0).astype(F32).astype(BF16)
        reach[:, at] = jnp.where(groups <= labels, jnp.ones((), BF16), jnp.zeros((), BF16))
        return carry

    lax.fori_loop(0, rows // part, mark, 0)
    if steps > 2:
        piece(2).start()

    def body(step, carry):
        at = pl.ds(pl.multiple_of(step * chunk, chunk), chunk)
        piece(step).wait()

        @pl.when(step + 3 < steps)
        def _():
            piece(step + 3).start()

        full = buf[at, :]
        hi = full.astype(BF16)
        lo = (full - hi.astype(F32)).astype(BF16)
        high[at, :] = hi
        low[at, :] = lo
        dims = (((1,), (1,)), ((), ()))
        out = lax.dot_general(coeffs, hi, dims, preferred_element_type=F32)
        out += lax.dot_general(coeffs, lo, dims, preferred_element_type=F32)
        values = unstack3(out, 3)
        per = chunk // LANES
        place = lin.at[:, pl.ds(pl.multiple_of(step * per, per), per)]
        for j in range(per):
            place[:, j, :] = values[:, j * LANES : (j + 1) * LANES]
        return carry

    lax.fori_loop(0, steps, body, 0)


def tally(mine, other, valid, died, reach, stats, weighted, spread, keep):
    total = mine[...] + other[...]
    weight = jnp.where(valid[...] > 0.0, jnp.exp(total[0]), 0.0)
    values = (weight, weight * total[1], weight * total[2], died[...])
    keep[0] = weight
    keep[1] = total[1]
    keep[2] = total[2]
    for k, value in enumerate(values):
        for part, piece in enumerate(split3(value)):
            spread[4 * part + k] = piece
        spread[12 + k] = jnp.zeros_like(value)
    steps = weight.shape[0]
    for j in range(steps):
        weighted[:, j * LANES : (j + 1) * LANES] = keep[:, j, :]
    lhs = jnp.concatenate([spread[:, j, :] for j in range(steps)], axis=1).astype(BF16)
    out = lax.dot_general(
        lhs, reach[...], (((1,), (1,)), ((), ())), preferred_element_type=F32
    )
    sums = unstack3(out, 4)
    for slot in range(stats.shape[0]):
        stats[slot] = sums


def second_pass(shards, scale, shard, stats, weighted, reach, high, low, out):
    me = shard[0]
    peers = stats.shape[0]
    each = peers // shards
    per_shard = []
    for s in range(shards):
        acc = stats[s * each]
        for p in range(1, each):
            acc = acc + stats[s * each + p]
        per_shard.append(acc)
    width = per_shard[0].shape[1]
    lane = lax.broadcasted_iota(jnp.int32, (1, width), 1)

    tail = jnp.zeros((4, 1), F32)
    tails = [None] * shards
    for s in reversed(range(shards)):
        tails[s] = tail
        tail = tail + per_shard[s][:, 0:1]

    def ratios_of(s):
        risk = per_shard[s] + tails[s]
        late = per_shard[s][3:4]
        died_grp = late - jnp.where(lane == width - 1, 0.0, pltpu.roll(late, width - 1, 1))
        risk0 = risk[0:1]
        return jnp.concatenate([died_grp / risk0, died_grp * risk[1:3] / (risk0 * risk0)], axis=0)

    chosen = jnp.zeros((3, width), F32)
    head = jnp.zeros((3, 1), F32)
    for s in range(shards):
        value = ratios_of(s)
        chosen = jnp.where(me == s, value, chosen)
        head = head + jnp.where(me > s, jnp.sum(value, axis=1, keepdims=True), 0.0)
    looked = unstack3(jnp.dot(stack3(chosen), reach[...], preferred_element_type=F32), 3) + head
    weight = weighted[0:1]
    proj = weighted[1:3]
    resid = weight * (proj * looked[0:1] - looked[1:3])
    lhs = stack3(resid)
    prod = jnp.dot(lhs, high[...], preferred_element_type=F32)
    prod += jnp.dot(lhs, low[...], preferred_element_type=F32)
    prod = unstack3(prod, 2) * scale
    for slot in range(out.shape[0]):
        out[slot] = prod


def per_device(covars, events, group, counts, beta, vecs):
    rows, cols = covars.shape
    shards = lax.axis_size("tm")
    peers = shards * lax.axis_size("loan")
    records = rows * peers
    chunk = min(1024, rows)
    dense = (rows // LANES, LANES)
    shard = lax.axis_index("tm").astype(jnp.int32)[None]
    hbm = pl.BlockSpec(memory_space=pltpu.HBM)
    vmem = pl.BlockSpec(memory_space=pltpu.VMEM)
    smem = pl.BlockSpec(memory_space=pltpu.SMEM)

    def arr(shape, dtype=F32):
        return jax.ShapeDtypeStruct(shape, dtype)

    def kept(shape, dtype=F32):
        return pltpu.VMEM(shape, dtype)

    lin, died, valid, reach, high, low = pl.pallas_call(
        functools.partial(first_pass, chunk),
        out_shape=(
            arr((3, *dense)), arr(dense), arr(dense),
            kept((G_SH, rows), BF16), kept((rows, cols), BF16), kept((rows, cols), BF16),
        ),
        in_specs=[hbm] * 3 + [smem] * 2 + [hbm] * 2,
        out_specs=(vmem,) * 6,
        scratch_shapes=[
            pltpu.VMEM((rows, cols), F32),
            pltpu.VMEM((1, cols), F32),
            pltpu.VMEM((2, cols), F32),
            pltpu.VMEM((1, rows), jnp.int32),
            pltpu.VMEM(dense, jnp.int32),
            pltpu.SemaphoreType.DMA((rows // chunk,)),
            pltpu.SemaphoreType.DMA((4,)),
        ],
        compiler_params=pltpu.CompilerParams(vmem_limit_bytes=24 << 20),
        name="first_pass",
    )(
        *(
            pltpu.with_memory_space_constraint(x, pltpu.HBM)
            for x in (covars, events.reshape(dense), group[None])
        ),
        counts,
        shard,
        *(pltpu.with_memory_space_constraint(x, pltpu.HBM) for x in (beta[None], vecs)),
    )

    pairs = [(i, i ^ 1) for i in range(2)]
    other = lax.ppermute(lin, "cov", pairs)

    stats, weighted = pl.pallas_call(
        tally,
        out_shape=(arr((peers, 4, G_SH)), arr((3, rows))),
        in_specs=[vmem] * 5,
        out_specs=(vmem,) * 2,
        scratch_shapes=[pltpu.VMEM((16, *dense), F32), pltpu.VMEM((3, *dense), F32)],
        compiler_params=pltpu.CompilerParams(vmem_limit_bytes=16 << 20),
        name="tally",
    )(lin, other, valid, died, reach)

    everyone = lax.all_to_all(stats, ("tm", "loan"), 0, 0)

    parts = pl.pallas_call(
        functools.partial(second_pass, shards, 1.0 / records),
        out_shape=arr((peers, 2, cols)),
        in_specs=[smem] + [vmem] * 5,
        out_specs=vmem,
        compiler_params=pltpu.CompilerParams(vmem_limit_bytes=16 << 20),
        name="second_pass",
    )(shard, everyone, weighted, reach, high, low)

    return jnp.sum(lax.all_to_all(parts, ("tm", "loan"), 0, 0), axis=0)


def solution(mesh):
    return jax.shard_map(
        per_device,
        mesh=mesh,
        in_specs=(
            P(("tm", "loan"), "cov"),
            P(("tm", "loan")),
            P(("tm", "loan")),
            P(("tm", "loan")),
            P("cov"),
            P(None, "cov"),
        ),
        out_specs=P(None, "cov"),
        check_vma=False,
    )
```

```python
import functools

import jax
import jax.numpy as jnp
from jax import lax
from jax.experimental import pallas as pl
from jax.experimental.pallas import tpu as pltpu
from jax.sharding import PartitionSpec as P

G_SH = 256
LANES = 128
BF16 = jnp.bfloat16
F32 = jnp.float32


def split3(x):
    hi = x.astype(BF16).astype(F32)
    rest = x - hi
    mid = rest.astype(BF16).astype(F32)
    return hi, mid, rest - mid


def stack3(x):
    used, width = x.shape
    rest = jnp.zeros((16 - 3 * used, width), F32)
    return jnp.concatenate([*split3(x), rest], axis=0).astype(BF16)


def unstack3(y, used):
    return (y[2 * used : 3 * used] + y[used : 2 * used]) + y[0:used]


def first_pass(
    chunk, covars, events, group, counts, shard, beta, vecs,
    lin, died, valid, reach, high, low,
    buf, beta_v, vecs_v, group_v, events_v, sems, small,
):
    rows = covars.shape[0]
    steps = rows // chunk
    copies = [
        pltpu.make_async_copy(group, group_v, small.at[0]),
        pltpu.make_async_copy(beta, beta_v, small.at[1]),
        pltpu.make_async_copy(vecs, vecs_v, small.at[2]),
        pltpu.make_async_copy(events, events_v, small.at[3]),
    ]
    for copy in copies:
        copy.start()

    def piece(step):
        at = pl.ds(pl.multiple_of(step * chunk, chunk), chunk)
        return pltpu.make_async_copy(covars.at[at], buf.at[at], sems.at[step])

    piece(0).start()
    pl.delay(500)
    if steps > 1:
        piece(1).start()
    for copy in copies:
        copy.wait()
    dense = (rows // LANES, LANES)
    index = lax.broadcasted_iota(jnp.int32, dense, 0) * LANES
    ok = index + lax.broadcasted_iota(jnp.int32, dense, 1) < counts[0]
    valid[...] = jnp.where(ok, 1.0, 0.0)
    died[...] = jnp.where(ok, events_v[...].astype(F32), 0.0)
    coeffs = stack3(jnp.concatenate([beta_v[...], vecs_v[...]], axis=0))
    base = shard[0] * G_SH
    part = min(512, chunk)

    def mark(step, carry):
        at = pl.ds(pl.multiple_of(step * part, part), part)
        labels = (group_v[:, at] - base).astype(F32).astype(BF16)
        groups = lax.broadcasted_iota(jnp.int32, (G_SH, part), 0).astype(F32).astype(BF16)
        reach[:, at] = jnp.where(groups <= labels, jnp.ones((), BF16), jnp.zeros((), BF16))
        return carry

    lax.fori_loop(0, rows // part, mark, 0)
    for step in range(2, min(4, steps)):
        piece(step).start()

    def body(step, carry):
        at = pl.ds(pl.multiple_of(step * chunk, chunk), chunk)
        piece(step).wait()

        @pl.when(step + 4 < steps)
        def _():
            piece(step + 4).start()

        full = buf[at, :]
        hi = full.astype(BF16)
        lo = (full - hi.astype(F32)).astype(BF16)
        high[at, :] = hi
        low[at, :] = lo
        dims = (((1,), (1,)), ((), ()))
        out = lax.dot_general(coeffs, hi, dims, preferred_element_type=F32)
        out += lax.dot_general(coeffs, lo, dims, preferred_element_type=F32)
        values = unstack3(out, 3)
        per = chunk // LANES
        place = lin.at[:, pl.ds(pl.multiple_of(step * per, per), per)]
        for j in range(per):
            place[:, j, :] = values[:, j * LANES : (j + 1) * LANES]
        return carry

    lax.fori_loop(0, steps, body, 0)


def tally(mine, other, valid, died, reach, stats, weighted, spread, keep):
    total = mine[...] + other[...]
    weight = jnp.where(valid[...] > 0.0, jnp.exp(total[0]), 0.0)
    values = (weight, weight * total[1], weight * total[2], died[...])
    keep[0] = weight
    keep[1] = total[1]
    keep[2] = total[2]
    for k, value in enumerate(values):
        for part, piece in enumerate(split3(value)):
            spread[4 * part + k] = piece
        spread[12 + k] = jnp.zeros_like(value)
    steps = weight.shape[0]
    for j in range(steps):
        weighted[:, j * LANES : (j + 1) * LANES] = keep[:, j, :]
    lhs = jnp.concatenate([spread[:, j, :] for j in range(steps)], axis=1).astype(BF16)
    out = lax.dot_general(
        lhs, reach[...], (((1,), (1,)), ((), ())), preferred_element_type=F32
    )
    sums = unstack3(out, 4)
    for slot in range(stats.shape[0]):
        stats[slot] = sums


def second_pass(shards, scale, shard, stats, weighted, reach, high, low, out):
    me = shard[0]
    peers = stats.shape[0]
    each = peers // shards
    per_shard = []
    for s in range(shards):
        acc = stats[s * each]
        for p in range(1, each):
            acc = acc + stats[s * each + p]
        per_shard.append(acc)
    width = per_shard[0].shape[1]
    lane = lax.broadcasted_iota(jnp.int32, (1, width), 1)

    tail = jnp.zeros((4, 1), F32)
    tails = [None] * shards
    for s in reversed(range(shards)):
        tails[s] = tail
        tail = tail + per_shard[s][:, 0:1]

    def ratios_of(s):
        risk = per_shard[s] + tails[s]
        late = per_shard[s][3:4]
        died_grp = late - jnp.where(lane == width - 1, 0.0, pltpu.roll(late, width - 1, 1))
        risk0 = risk[0:1]
        return jnp.concatenate([died_grp / risk0, died_grp * risk[1:3] / (risk0 * risk0)], axis=0)

    chosen = jnp.zeros((3, width), F32)
    head = jnp.zeros((3, 1), F32)
    for s in range(shards):
        value = ratios_of(s)
        chosen = jnp.where(me == s, value, chosen)
        head = head + jnp.where(me > s, jnp.sum(value, axis=1, keepdims=True), 0.0)
    looked = unstack3(jnp.dot(stack3(chosen), reach[...], preferred_element_type=F32), 3) + head
    weight = weighted[0:1]
    proj = weighted[1:3]
    resid = weight * (proj * looked[0:1] - looked[1:3])
    lhs = stack3(resid)
    prod = jnp.dot(lhs, high[...], preferred_element_type=F32)
    prod += jnp.dot(lhs, low[...], preferred_element_type=F32)
    prod = unstack3(prod, 2) * scale
    for slot in range(out.shape[0]):
        out[slot] = prod


def per_device(covars, events, group, counts, beta, vecs):
    rows, cols = covars.shape
    shards = lax.axis_size("tm")
    peers = shards * lax.axis_size("loan")
    records = rows * peers
    chunk = min(1024, rows)
    dense = (rows // LANES, LANES)
    shard = lax.axis_index("tm").astype(jnp.int32)[None]
    hbm = pl.BlockSpec(memory_space=pltpu.HBM)
    vmem = pl.BlockSpec(memory_space=pltpu.VMEM)
    smem = pl.BlockSpec(memory_space=pltpu.SMEM)

    def arr(shape, dtype=F32):
        return jax.ShapeDtypeStruct(shape, dtype)

    def kept(shape, dtype=F32):
        return pltpu.VMEM(shape, dtype)

    lin, died, valid, reach, high, low = pl.pallas_call(
        functools.partial(first_pass, chunk),
        out_shape=(
            arr((3, *dense)), arr(dense), arr(dense),
            kept((G_SH, rows), BF16), kept((rows, cols), BF16), kept((rows, cols), BF16),
        ),
        in_specs=[hbm] * 3 + [smem] * 2 + [hbm] * 2,
        out_specs=(vmem,) * 6,
        scratch_shapes=[
            pltpu.VMEM((rows, cols), F32),
            pltpu.VMEM((1, cols), F32),
            pltpu.VMEM((2, cols), F32),
            pltpu.VMEM((1, rows), jnp.int32),
            pltpu.VMEM(dense, jnp.int32),
            pltpu.SemaphoreType.DMA((rows // chunk,)),
            pltpu.SemaphoreType.DMA((4,)),
        ],
        compiler_params=pltpu.CompilerParams(vmem_limit_bytes=24 << 20),
        name="first_pass",
    )(
        *(
            pltpu.with_memory_space_constraint(x, pltpu.HBM)
            for x in (covars, events.reshape(dense), group[None])
        ),
        counts,
        shard,
        *(pltpu.with_memory_space_constraint(x, pltpu.HBM) for x in (beta[None], vecs)),
    )

    pairs = [(i, i ^ 1) for i in range(2)]
    other = lax.ppermute(lin, "cov", pairs)

    stats, weighted = pl.pallas_call(
        tally,
        out_shape=(arr((peers, 4, G_SH)), arr((3, rows))),
        in_specs=[vmem] * 5,
        out_specs=(vmem,) * 2,
        scratch_shapes=[pltpu.VMEM((16, *dense), F32), pltpu.VMEM((3, *dense), F32)],
        compiler_params=pltpu.CompilerParams(vmem_limit_bytes=16 << 20),
        name="tally",
    )(lin, other, valid, died, reach)

    everyone = lax.all_to_all(stats, ("tm", "loan"), 0, 0)

    parts = pl.pallas_call(
        functools.partial(second_pass, shards, 1.0 / records),
        out_shape=arr((peers, 2, cols)),
        in_specs=[smem] + [vmem] * 5,
        out_specs=vmem,
        compiler_params=pltpu.CompilerParams(vmem_limit_bytes=16 << 20),
        name="second_pass",
    )(shard, everyone, weighted, reach, high, low)

    return jnp.sum(lax.all_to_all(parts, ("tm", "loan"), 0, 0), axis=0)


def solution(mesh):
    return jax.shard_map(
        per_device,
        mesh=mesh,
        in_specs=(
            P(("tm", "loan"), "cov"),
            P(("tm", "loan")),
            P(("tm", "loan")),
            P(("tm", "loan")),
            P("cov"),
            P(None, "cov"),
        ),
        out_specs=P(None, "cov"),
        check_vma=False,
    )
```
